1024 devices in a mesh: ctx: 128 (over y, z), head: 8 (over x, core).
Axes of the slice: x: 4, y: 8, z: 16, core: 2. Of those that a mesh axis runs over, the one named last changes fastest.
Arguments:
- queries: bfloat16 [32768, 4096], P('ctx', 'head'), may hold values from -8 to 8
- keys: bfloat16 [32768, 1024], P('ctx', 'head'), may hold values from -6 to 6
- values: bfloat16 [32768, 1024], P('ctx', 'head'), may hold values from -6 to 6
- segment_ids: int32 [32768], P('ctx'), may hold values from 0 to 31, never falling along the last dimension, each value on 1 to 1792 neighbouring positions
- out_weight: bfloat16 [4096, 4096], P('head'), may hold values from -0.125 to 0.125
Outputs:
- mixed: bfloat16 [32768, 4096], P('ctx', 'head')
The draws below stay inside these ranges and needn't reach their ends.
Inputs may be any that keep to these rules, and one draw needn't show every extreme that they name: `segment_ids`: documents are contiguous runs of tokens; none is longer than 1792 tokens and one is exactly that long.
All inputs are finite; a program needn't handle non-finite values.
Results may differ from the reference program's by a relative error of at most 0.015.
Values may be sent and summed in bfloat16 or wider, within the bound.
A program may use at most 32 MiB of HBM per device.

```python
import math
import jax
import jax.numpy as jnp
import numpy as np
from jax import lax

D = 4096
HEADS = 32
KV_HEADS = 8
HEAD_DIM = 128
SEGS = 32
SEQ = 32768
DOC_MAX = 1792


def draw_queries(key, part):
    inner = jax.random.fold_in(key, 3)
    result = jnp.clip(2.0 * jax.random.normal(inner, (SEQ, HEADS * HEAD_DIM), jnp.float32), -8.0, 8.0)
    return result.astype(jnp.bfloat16)


def draw_keys(key, part):
    inner = jax.random.fold_in(key, 5)
    result = jnp.clip(jax.random.normal(inner, (SEQ, KV_HEADS, HEAD_DIM), jnp.float32), -6.0, 6.0)
    return result.reshape(SEQ, KV_HEADS * HEAD_DIM).astype(jnp.bfloat16)


def with_spikes(values, own_key, source, target, blocks, factor):
    owner, partner = [(jnp.arange(values.shape[axis_at]) // (values.shape[axis_at] // blocks)).reshape([-1 if axis == axis_at else 1 for axis in range(values.ndim)]) for axis_at in (source, target)]
    chosen = jax.random.permutation(own_key, blocks)[partner]
    strong = (owner == chosen) | (owner == (partner + blocks // 2) % blocks)
    return jnp.where(strong, factor * values, values)


def levels(rng, extent, cuts, low, largest):
    def one(axis_at, shards_of):
        draws = jax.random.uniform(jax.random.fold_in(jax.random.fold_in(rng, 6), axis_at), (shards_of,), jnp.float32, low / len(cuts), largest / len(cuts))
        return jnp.repeat(jnp.exp(draws), extent[axis_at] // shards_of).reshape((-1,) + (1,) * (len(extent) - axis_at - 1))

    loudness = one(*cuts[0])
    for cut in cuts[1:]:
        loudness = loudness * one(*cut)
    return loudness


def split_up(amount, total, most, lean):
    weights = [(1 << 20) // math.isqrt(grade ** lean) + 1 for grade in range(2, amount + 1)]
    rest, counts = total - most - (amount - 1), [1] * (amount - 1)
    while rest > 0:
        candidates = [i for i in range(amount - 1) if counts[i] < most]
        pool, budget = sum([weights[i] for i in candidates]), rest
        for i in candidates:
            extra = min(most - counts[i], max(1, budget * weights[i] // pool), rest)
            counts[i] = counts[i] + extra
            rest = rest - extra
    return np.array([most] + counts)


def ragged_sizes(rng, count, total, most, lean):
    if count == 2:
        one = jax.random.randint(rng, (), max(1, total - most), min(most, total - 1) + 1)
        return jnp.stack([one, total - one])
    sizes = jnp.asarray(split_up(count, total, most, lean), jnp.int32)
    twos = (count - 1) // 2
    source_of, sink = sizes[1:1 + 2 * twos:2], sizes[2:2 + 2 * twos:2]
    margin = jnp.minimum(source_of - 1, most - sink)
    moved = jax.random.randint(jax.random.fold_in(rng, 1), (twos,), 0, 1 << 20) % (margin + 1)
    sizes = sizes.at[1:1 + 2 * twos:2].set(source_of - moved).at[2:2 + 2 * twos:2].set(sink + moved)
    return sizes[jax.random.permutation(jax.random.fold_in(rng, 2), count)]


def normal_values(key, dims, spread, most, shards=(), held_as=jnp.bfloat16):
    entries = jax.random.normal(key, dims, jnp.float32) * spread
    if len(shards) > 0:
        entries = levels(key, dims, shards, -0.22, 0.18) * entries
    return jnp.clip(entries, min=-most, max=most).astype(held_as)


def noise_with(stream_key, extent, spread, bound, cuts, heavy, kind=jnp.bfloat16):
    drawn = spread * jax.random.normal(stream_key, extent, jnp.float32)
    if cuts:
        drawn = drawn * levels(stream_key, extent, cuts, -0.22, 0.18)
    return jnp.clip(with_spikes(drawn, jax.random.fold_in(stream_key, 3), *heavy), -bound, bound).astype(kind)


def setup_inputs(seed: int = 0) -> dict:
    key_list = jax.random.split(jax.random.key(seed), 6)
    return {
        "queries": draw_queries(jax.random.fold_in(key_list[5], 71), 0),
        "keys": draw_keys(jax.random.fold_in(key_list[5], 71), 0),
        "values": normal_values(key_list[2], (SEQ, KV_HEADS * HEAD_DIM), 1.0, 6.0, ((0, 128), (1, 8))),
        "segment_ids": jnp.searchsorted(jnp.cumsum(ragged_sizes(key_list[3], SEGS, SEQ, DOC_MAX, 1)), jnp.arange(SEQ), side="right").astype(jnp.int32),
        "out_weight": noise_with(key_list[4], (D, D), D ** -0.5, 0.125, ((0, 8),), (0, 1, 8, 2.0)),
    }


def reference(queries, keys, values, segment_ids, out_weight):
    block = math.gcd(SEQ, 256)
    width = min(SEQ, DOC_MAX + block)
    groups = HEADS // KV_HEADS
    scale = 1.0 / math.sqrt(HEAD_DIM)

    def one_block(index):
        start = (index * block).astype(jnp.int32)
        kstart = jnp.clip(start + block - width, 0, SEQ - width).astype(jnp.int32)
        query = lax.dynamic_slice_in_dim(queries, start, block, 0).astype(jnp.float32)
        query = query.reshape(block, KV_HEADS, groups, HEAD_DIM)
        keyset = lax.dynamic_slice_in_dim(keys, kstart, width, 0).astype(jnp.float32)
        keyset = keyset.reshape(width, KV_HEADS, HEAD_DIM)
        valset = lax.dynamic_slice_in_dim(values, kstart, width, 0).astype(jnp.float32)
        valset = valset.reshape(width, KV_HEADS, HEAD_DIM)
        qpos = start + jnp.arange(block, dtype=jnp.int32)
        kpos = kstart + jnp.arange(width, dtype=jnp.int32)
        qseg = lax.dynamic_slice_in_dim(segment_ids, start, block, 0)
        kseg = lax.dynamic_slice_in_dim(segment_ids, kstart, width, 0)
        visible = (kpos[None, :] <= qpos[:, None]) & (kseg[None, :] == qseg[:, None])
        scores = jnp.einsum('qgrd,kgd->grqk', query, keyset) * scale
        top = lax.optimization_barrier(jnp.max(jnp.where(visible, scores, -1e+30), axis=-1))
        weights = jnp.where(visible, jnp.exp(scores - top[..., None]), 0.0)
        total = lax.optimization_barrier(jnp.sum(weights, axis=-1))
        rounded = lax.optimization_barrier(weights.astype(jnp.bfloat16)).astype(jnp.float32)
        summed = jnp.einsum('grqk,kgd->qgrd', rounded, valset)
        attended = summed / jnp.transpose(total, (2, 0, 1))[..., None]
        return attended.reshape(block, HEADS * HEAD_DIM).astype(jnp.bfloat16)
    blocks = lax.map(one_block, jnp.arange(SEQ // block, dtype=jnp.int32))
    attended = blocks.reshape(SEQ, HEADS * HEAD_DIM)
    return jnp.dot(attended, out_weight, preferred_element_type=jnp.float32).astype(jnp.bfloat16)
```

```python
import functools
import math

import jax
import jax.numpy as jnp
from jax import lax
from jax.experimental import pallas as pl
from jax.experimental.pallas import tpu as pltpu
from jax.sharding import PartitionSpec as P

HEAD_DIM = 128
DOC_MAX = 1792
MESH = pl.DeviceIdType.MESH
NEG = -1e30
F32 = jnp.float32
BF16 = jnp.bfloat16


def kernel(hops, n_ctx, n_x, q_hbm, k_hbm, v_hbm, s_hbm, w_hbm, o_ref,
           q_own, k_own, v_own, s_own, kbuf, vbuf, sbuf, w_buf, att, acc, top,
           opp, to_p, to_m, relay_p, relay_m, from_m, from_p,
           own_sem, wl_sem, ws_sem, wr_sem, hs_sem, hr_sem, as_sem, ar_sem, xs_sem, xr_sem):
    tokens, width = q_own.shape
    heads = width // HEAD_DIM
    half = tokens // 2
    place = lax.axis_index("ctx")
    head = lax.axis_index("head")
    x, core = head // 2, head % 2
    nxt, prv = lax.rem(place + 1, n_ctx), lax.rem(place + n_ctx - 1, n_ctx)
    partner = (place, x * 2 + (1 - core))
    x_p = (place, lax.rem(x + 1, n_x) * 2 + core)
    x_m = (place, lax.rem(x + n_x - 1, n_x) * 2 + core)
    c = math.log2(math.e) / math.sqrt(HEAD_DIM)

    def remote(src, dst, send, recv, device):
        return pltpu.make_async_remote_copy(
            src_ref=src, dst_ref=dst, send_sem=send, recv_sem=recv,
            device_id=device, device_id_type=MESH)

    local = [pltpu.make_async_copy(src, dst, own_sem.at[i]) for i, (src, dst) in enumerate(
        [(s_hbm, s_own), (k_hbm, k_own), (q_hbm, q_own), (v_hbm, v_own)])]
    for copy in local:
        copy.start()

    barrier = pltpu.get_barrier_semaphore()
    for device in ((nxt, head), (prv, head), partner, x_p, x_m):
        pl.semaphore_signal(barrier, inc=1, device_id=device, device_id_type=MESH)
    pl.semaphore_wait(barrier, 5)

    def own_hop(which):
        src = (s_hbm, k_hbm, v_hbm)[which]
        dst = (sbuf, kbuf, vbuf)[which].at[0]
        return remote(src, dst, hs_sem.at[0, which], hr_sem.at[0, which], (nxt, head))

    def hop(which, step):
        buf = (sbuf, kbuf, vbuf)[which]
        return remote(buf.at[step - 1], buf.at[step], hs_sem.at[step, which],
                      hr_sem.at[step, which], (nxt, head))

    def arrived(which, step):
        buf = (sbuf, kbuf, vbuf)[which]
        return remote(buf.at[step], buf.at[step], hs_sem.at[step, which],
                      hr_sem.at[step, which], (nxt, head))

    for which in range(3):
        own_hop(which).start()

    def w_local(r):
        col = pl.multiple_of((lax.rem(x + r, n_x) * 2 + core) * width, width)
        return pltpu.make_async_copy(
            w_hbm.at[:, pl.ds(col, width)], w_buf.at[r, 0:width, :], wl_sem.at[r])

    def w_remote(r):
        col = pl.multiple_of((lax.rem(x + r, n_x) * 2 + (1 - core)) * width, width)
        return remote(w_hbm.at[:, pl.ds(col, width)], w_buf.at[r, width:2 * width, :],
                      ws_sem.at[r], wr_sem.at[r], partner)

    for r in range(n_x):
        w_local(r).start()
        w_remote(r).start()

    for copy in local:
        copy.wait()

    ones = jnp.ones((tokens, HEAD_DIM), BF16)
    k_iota = lax.broadcasted_iota(jnp.int32, (tokens, tokens), 1)
    q_iota = lax.broadcasted_iota(jnp.int32, (tokens, tokens), 0)
    seg_row = s_own[...].astype(F32)
    first = jnp.min(seg_row, axis=1, keepdims=True)
    count_own = jnp.sum(jnp.where(seg_row == first, 1.0, 0.0), axis=1, keepdims=True).astype(jnp.int32)

    def scores(h, keys):
        return lax.dot_general(q_own[:, h * HEAD_DIM:(h + 1) * HEAD_DIM], keys,
                               (((1,), (1,)), ((), ())), preferred_element_type=F32)

    seg_col = jnp.transpose(jnp.broadcast_to(seg_row, (HEAD_DIM, tokens)))
    seg_col = jnp.concatenate([seg_col] * (tokens // HEAD_DIM), axis=1)
    visible = (seg_col == seg_row) & (k_iota <= q_iota)
    keys = k_own[...]
    v_ext = jnp.concatenate([v_own[...], ones], axis=1)
    for h in range(heads):
        s = jnp.where(visible, scores(h, keys), NEG)
        m = jnp.max(s, axis=1, keepdims=True)
        p = jnp.exp2((s - m) * c)
        acc[h] = jnp.dot(p.astype(BF16), v_ext, preferred_element_type=F32)
        top[h] = jnp.broadcast_to(m, (tokens, HEAD_DIM))

    def absorb(step):
        ids = sbuf[step].astype(F32)
        match = jnp.where(ids == first, 1.0, 0.0)
        count = jnp.sum(match, axis=1, keepdims=True).astype(jnp.int32)
        count = jnp.where(place > step, count, 0)
        visible = (q_iota < count_own) & (k_iota >= tokens - count)
        keys = kbuf[step]
        v_ext = jnp.concatenate([vbuf[step], ones], axis=1)
        for h in range(heads):
            s = jnp.where(visible, scores(h, keys), NEG)
            m_old = top[h][:, 0:1]
            m = jnp.maximum(m_old, jnp.max(s, axis=1, keepdims=True))
            p = jnp.exp2((s - m) * c)
            alpha = jnp.exp2((m_old - m) * c)
            acc[h] = acc[h] * alpha + jnp.dot(p.astype(BF16), v_ext, preferred_element_type=F32)
            top[h] = jnp.broadcast_to(m, (tokens, HEAD_DIM))

    def turn(step, _):
        for which in range(3):
            arrived(which, step - 1).wait_recv()
            hop(which, step).start()
        absorb(step - 1)
        return 0

    lax.fori_loop(1, hops, turn, 0)
    for which in range(3):
        arrived(which, hops - 1).wait_recv()
    absorb(hops - 1)

    def give(h):
        mine = att.at[:, h * HEAD_DIM:(h + 1) * HEAD_DIM]
        theirs = att.at[:, width + h * HEAD_DIM:width + (h + 1) * HEAD_DIM]
        return remote(mine, theirs, as_sem.at[h], ar_sem.at[h], partner)

    for h in range(heads):
        done = acc[h]
        att[:, h * HEAD_DIM:(h + 1) * HEAD_DIM] = (
            done[:, :HEAD_DIM] / done[:, HEAD_DIM:]).astype(BF16)
        give(h).start()

    for r in range(n_x):
        w_local(r).wait()
        w_remote(r).wait()
    for h in range(heads):
        give(h).wait()

    top_rows, low_rows = slice(0, half), slice(half, tokens)

    def project(rows, r):
        return jnp.dot(att[rows, :], w_buf[r], preferred_element_type=F32)

    opp_p = remote(opp.at[top_rows, :], relay_p, xs_sem.at[0], xr_sem.at[0], x_p)
    opp_m = remote(opp.at[low_rows, :], relay_m, xs_sem.at[1], xr_sem.at[1], x_m)
    plain_p = remote(to_p.at[low_rows, :], from_m.at[low_rows, :], xs_sem.at[2], xr_sem.at[2], x_p)
    plain_m = remote(to_m.at[top_rows, :], from_p.at[top_rows, :], xs_sem.at[3], xr_sem.at[3], x_m)
    sum_p = remote(to_p.at[top_rows, :], from_m.at[top_rows, :], xs_sem.at[4], xr_sem.at[4], x_p)
    sum_m = remote(to_m.at[low_rows, :], from_p.at[low_rows, :], xs_sem.at[5], xr_sem.at[5], x_m)

    opp[top_rows, :] = project(top_rows, 2).astype(BF16)
    opp_p.start()
    opp[low_rows, :] = project(low_rows, 2).astype(BF16)
    opp_m.start()
    to_p[low_rows, :] = project(low_rows, 1).astype(BF16)
    plain_p.start()
    to_m[top_rows, :] = project(top_rows, 3).astype(BF16)
    plain_m.start()
    mine_p = project(top_rows, 1)
    opp_p.wait_recv()
    to_p[top_rows, :] = (mine_p + relay_p[...].astype(F32)).astype(BF16)
    sum_p.start()
    mine_m = project(low_rows, 3)
    opp_m.wait_recv()
    to_m[low_rows, :] = (mine_m + relay_m[...].astype(F32)).astype(BF16)
    sum_m.start()
    own_top = project(top_rows, 0)
    own_low = project(low_rows, 0)
    plain_p.wait_recv()
    plain_m.wait_recv()
    sum_p.wait_recv()
    o_ref[top_rows, :] = (own_top + from_m[top_rows, :].astype(F32)
                          + from_p[top_rows, :].astype(F32)).astype(BF16)
    sum_m.wait_recv()
    o_ref[low_rows, :] = (own_low + from_m[low_rows, :].astype(F32)
                          + from_p[low_rows, :].astype(F32)).astype(BF16)
    for copy in (opp_p, opp_m, plain_p, plain_m, sum_p, sum_m):
        copy.wait_send()
    for which in range(3):
        own_hop(which).wait_send()

    def settle(step, _):
        for which in range(3):
            hop(which, step).wait_send()
        return 0

    lax.fori_loop(1, hops, settle, 0)


def solution(mesh):
    n_ctx, n_head = mesh.shape["ctx"], mesh.shape["head"]
    n_x = n_head // 2

    def body(queries, keys, values, segment_ids, out_weight):
        tokens, width = queries.shape
        heads = width // HEAD_DIM
        hops = min(-(-(DOC_MAX - 1) // tokens), n_ctx - 1)
        half = tokens // 2
        any_space = pl.BlockSpec(memory_space=pl.ANY)
        dma = pltpu.SemaphoreType.DMA
        return pl.pallas_call(
            functools.partial(kernel, hops, n_ctx, n_x),
            out_shape=jax.ShapeDtypeStruct((tokens, width), BF16),
            in_specs=[any_space] * 5,
            out_specs=pl.BlockSpec(memory_space=pltpu.VMEM),
            scratch_shapes=[
                pltpu.VMEM((tokens, width), BF16),
                pltpu.VMEM((tokens, HEAD_DIM), BF16),
                pltpu.VMEM((tokens, HEAD_DIM), BF16),
                pltpu.VMEM((1, tokens), jnp.int32),
                pltpu.VMEM((hops, tokens, HEAD_DIM), BF16),
                pltpu.VMEM((hops, tokens, HEAD_DIM), BF16),
                pltpu.VMEM((hops, 1, tokens), jnp.int32),
                pltpu.VMEM((n_x, 2 * width, width), BF16),
                pltpu.VMEM((tokens, 2 * width), BF16),
                pltpu.VMEM((heads, tokens, 2 * HEAD_DIM), F32),
                pltpu.VMEM((heads, tokens, HEAD_DIM), F32),
                pltpu.VMEM((tokens, width), BF16),
                pltpu.VMEM((tokens, width), BF16),
                pltpu.VMEM((tokens, width), BF16),
                pltpu.VMEM((half, width), BF16),
                pltpu.VMEM((half, width), BF16),
                pltpu.VMEM((tokens, width), BF16),
                pltpu.VMEM((tokens, width), BF16),
                dma((4,)),
                dma((n_x,)), dma((n_x,)), dma((n_x,)),
                dma((hops, 3)), dma((hops, 3)),
                dma((heads,)), dma((heads,)),
                dma((6,)), dma((6,)),
            ],
            compiler_params=pltpu.CompilerParams(collective_id=0, has_side_effects=True),
        )(queries, keys, values, segment_ids.reshape(1, tokens), out_weight)

    in_specs = (P("ctx", "head"), P("ctx", "head"), P("ctx", "head"), P("ctx"), P("head", None))
    return jax.shard_map(body, mesh=mesh, in_specs=in_specs, out_specs=P("ctx", "head"), check_vma=False)
```

```python
import functools
import math

import jax
import jax.numpy as jnp
from jax import lax
from jax.experimental import pallas as pl
from jax.experimental.pallas import tpu as pltpu
from jax.sharding import PartitionSpec as P

HEAD_DIM = 128
DOC_MAX = 1792
RING = 16
PIECES = 2
MESH = pl.DeviceIdType.MESH
NEG = -1e30
F32 = jnp.float32
BF16 = jnp.bfloat16


def kernel(hops, n_ctx, n_x, q_hbm, k_hbm, v_hbm, s_hbm, w_hbm, o_ref,
           q_own, k_own, v_own, s_own, kbuf, vbuf, sbuf, w_buf, att, acc, top,
           opp, to_p, to_m, relay_p, relay_m, from_m, from_p,
           via_s, via_k, via_v, wts, fade,
           own_sem, wl_sem, ws_sem, wr_sem, hs_sem, hr_sem, as_sem, ar_sem, xs_sem, xr_sem,
           ds_sem, dr_sem, es_sem):
    tokens, width = q_own.shape
    heads = width // HEAD_DIM
    half = tokens // 2
    place = lax.axis_index("ctx")
    head = lax.axis_index("head")
    x, core = head // 2, head % 2
    nxt, prv = lax.rem(place + 1, n_ctx), lax.rem(place + n_ctx - 1, n_ctx)
    n_row = max(n_ctx // RING, 1)
    row, col = place // RING, lax.rem(place, RING)
    detour = hops == 7 and n_ctx % RING == 0 and n_row > 1

    def spot(turns, where):
        return (lax.rem(row + turns + n_row, n_row) * RING + where, head)

    partner = (place, x * 2 + (1 - core))
    x_p = (place, lax.rem(x + 1, n_x) * 2 + core)
    x_m = (place, lax.rem(x + n_x - 1, n_x) * 2 + core)
    c = math.log2(math.e) / math.sqrt(HEAD_DIM)

    def remote(src, dst, send, recv, device):
        return pltpu.make_async_remote_copy(
            src_ref=src, dst_ref=dst, send_sem=send, recv_sem=recv,
            device_id=device, device_id_type=MESH)

    local = [pltpu.make_async_copy(src, dst, own_sem.at[i]) for i, (src, dst) in enumerate(
        [(s_hbm, s_own), (k_hbm, k_own), (q_hbm, q_own), (v_hbm, v_own)])]
    for copy in local:
        copy.start()

    barrier = pltpu.get_barrier_semaphore()

    def greet(device):
        pl.semaphore_signal(barrier, inc=1, device_id=device, device_id_type=MESH)

    for device in ((prv, head), partner, x_p, x_m):
        greet(device)
    if detour:
        for where, sources in ((5, ((-1, 9),)), (6, ((-1, 10),)), (0, ((0, 5), (0, 1))), (1, ((0, 6),))):
            @pl.when(col == where)
            def _():
                for source in sources:
                    greet(spot(*source))
    if detour:
        further = (col == 9) | (col == 10) | (col == 5) | (col == 6) | (col == 1)
        pl.semaphore_wait(barrier, jnp.where(further, 5, 4))
    else:
        pl.semaphore_wait(barrier, 4)

    piece = tokens // PIECES
    parts = 1 + 2 * PIECES

    def part(refs, which, *slot):
        if which == 0:
            return refs[0].at[slot] if slot else refs[0]
        at = (which - 1) % PIECES * piece
        return refs[1 + (which - 1) // PIECES].at[(*slot, slice(at, at + piece), slice(None))]

    given, slots, via = (s_hbm, k_hbm, v_hbm), (sbuf, kbuf, vbuf), (via_s, via_k, via_v)

    def own_hop(which):
        return remote(part(given, which), part(slots, which, 0), hs_sem.at[0, which],
                      hr_sem.at[0, which], (nxt, head))

    def hop(which, step):
        return remote(part(slots, which, step - 1), part(slots, which, step), hs_sem.at[step, which],
                      hr_sem.at[step, which], (nxt, head))

    def arrived(which, step):
        return remote(part(slots, which, step), part(slots, which, step), hs_sem.at[step, which],
                      hr_sem.at[step, which], (nxt, head))

    def leave(which, where):
        return remote(part(given, which), part(via, which), ds_sem.at[which], dr_sem.at[which],
                      spot(1, where))

    def pass_on(which, where):
        return remote(part(via, which), part(slots, which, 6), es_sem.at[which], hr_sem.at[6, which],
                      spot(0, where))

    def pass_last(which):
        return remote(part(slots, which, 6), part(slots, which, 5), es_sem.at[which],
                      hr_sem.at[5, which], spot(0, 0))

    @pl.when(place < n_ctx - 1)
    def _():
        for which in range(parts):
            own_hop(which).start()

    if detour:
        for here, where in ((9, 5), (10, 6)):
            @pl.when((col == here) & (row < n_row - 1))
            def _():
                for which in range(parts):
                    leave(which, where).start()

    def w_local(r):
        col = pl.multiple_of((lax.rem(x + r, n_x) * 2 + core) * width, width)
        return pltpu.make_async_copy(
            w_hbm.at[:, pl.ds(col, width)], w_buf.at[r, 0:width, :], wl_sem.at[r])

    def w_remote(r):
        col = pl.multiple_of((lax.rem(x + r, n_x) * 2 + (1 - core)) * width, width)
        return remote(w_hbm.at[:, pl.ds(col, width)], w_buf.at[r, width:2 * width, :],
                      ws_sem.at[r], wr_sem.at[r], partner)

    for r in range(n_x):
        w_local(r).start()
        w_remote(r).start()

    for copy in local:
        copy.wait()

    ones = jnp.ones((tokens, HEAD_DIM), BF16)
    k_iota = lax.broadcasted_iota(jnp.int32, (tokens, tokens), 1)
    q_iota = lax.broadcasted_iota(jnp.int32, (tokens, tokens), 0)
    seg_row = s_own[...].astype(F32)
    first = jnp.min(seg_row, axis=1, keepdims=True)
    count_own = jnp.sum(jnp.where(seg_row == first, 1.0, 0.0), axis=1, keepdims=True).astype(jnp.int32)

    def scores(h, keys):
        return lax.dot_general(q_own[:, h * HEAD_DIM:(h + 1) * HEAD_DIM], keys,
                               (((1,), (1,)), ((), ())), preferred_element_type=F32)

    def blank(step, _):
        kbuf[step] = jnp.zeros((tokens, HEAD_DIM), BF16)
        vbuf[step] = jnp.zeros((tokens, HEAD_DIM), BF16)
        sbuf[step] = jnp.full((1, tokens), -1, jnp.int32)
        return 0

    lax.fori_loop(jnp.minimum(place, hops), hops, blank, 0)

    seg_col = jnp.transpose(jnp.broadcast_to(seg_row, (HEAD_DIM, tokens)))
    seg_col = jnp.concatenate([seg_col] * (tokens // HEAD_DIM), axis=1)
    visible = (seg_col == seg_row) & (k_iota <= q_iota)
    keys = k_own[...]
    v_ext = jnp.concatenate([v_own[...], ones], axis=1)
    for h in range(heads):
        s = jnp.where(visible, scores(h, keys), NEG)
        m = jnp.max(s, axis=1, keepdims=True)
        p = jnp.exp2((s - m) * c)
        acc[h] = jnp.dot(p.astype(BF16), v_ext, preferred_element_type=F32)
        top[h] = jnp.broadcast_to(m, (tokens, HEAD_DIM))

    def weigh(step, which_heads):
        ids = sbuf[step].astype(F32)
        count = jnp.sum(jnp.where(ids == first, 1.0, 0.0), axis=1, keepdims=True).astype(jnp.int32)
        count = jnp.where(place > step, count, 0)
        start = jnp.where(q_iota[:, 0:1] < count_own, tokens - count, tokens)
        keys = kbuf[step]
        for h in which_heads:
            s = jnp.where(k_iota >= start, scores(h, keys), NEG)
            m_old = top[h][:, 0:1]
            m = jnp.maximum(m_old, jnp.max(s, axis=1, keepdims=True))
            wts[h] = jnp.exp2((s - m) * c).astype(BF16)
            fade[h] = jnp.broadcast_to(jnp.exp2((m_old - m) * c), (tokens, HEAD_DIM))
            top[h] = jnp.broadcast_to(m, (tokens, HEAD_DIM))

    def gather(step, h):
        v_ext = jnp.concatenate([vbuf[step], ones], axis=1)
        return acc[h] * fade[h][:, 0:1] + jnp.dot(wts[h], v_ext, preferred_element_type=F32)

    def gather_all(step, which_heads):
        for h in which_heads:
            acc[h] = gather(step, h)

    def onward(step):
        going = (place >= step) & (place < n_ctx - 1)
        if detour:
            going &= jnp.logical_not(((col == RING - 1) & (step >= 5)) | ((col == 0) & (step == 6)))
        return going

    lower, upper = range(heads // 2), range(heads // 2, heads)

    def turn(step, after):
        for which in range(parts):
            @pl.when(place >= step)
            def _():
                arrived(which, step - 1).wait_recv()

            @pl.when(onward(step))
            def _():
                hop(which, step).start()
            after(which)
        if detour:
            for here, where in ((5, 0), (6, 1)):
                @pl.when((step == 4) & (col == here) & (row > 0))
                def _():
                    for which in range(parts):
                        leave(which, where).wait_recv()
                        pass_on(which, where).start()

            @pl.when((step == 4) & (col == 1) & (row > 0))
            def _():
                for which in range(parts):
                    arrived(which, 6).wait_recv()
                    pass_last(which).start()

    def first_turn(which):
        if which == PIECES + 1:
            weigh(0, lower)
        if which == parts - 1:
            weigh(0, upper)

    turn(1, first_turn)

    def later(step, _):
        def after(which):
            if which == 1:
                gather_all(step - 2, lower)
            if which == PIECES:
                gather_all(step - 2, upper)
            if which == PIECES + 1:
                weigh(step - 1, lower)
            if which == parts - 1:
                weigh(step - 1, upper)

        turn(step, after)
        return 0

    lax.fori_loop(2, hops, later, 0)
    waits = place >= hops
    if detour:
        waits &= col != 1
    if hops > 1:
        gather_all(hops - 2, range(heads))
    for wanted in (range(0, PIECES + 1), range(PIECES + 1, parts)):
        @pl.when(waits)
        def _():
            for which in wanted:
                arrived(which, hops - 1).wait_recv()
        if 0 in wanted and hops > 1:
            weigh(hops - 1, range(heads))

    def give(h):
        mine = att.at[:, h * HEAD_DIM:(h + 1) * HEAD_DIM]
        theirs = att.at[:, width + h * HEAD_DIM:width + (h + 1) * HEAD_DIM]
        return remote(mine, theirs, as_sem.at[h], ar_sem.at[h], partner)

    def finish(h, done):
        att[:, h * HEAD_DIM:(h + 1) * HEAD_DIM] = (
            done[:, :HEAD_DIM] / done[:, HEAD_DIM:]).astype(BF16)
        give(h).start()

    for h in range(heads):
        finish(h, gather(hops - 1, h))

    for r in range(n_x):
        w_local(r).wait()
        w_remote(r).wait()
    for h in range(heads):
        give(h).wait()

    top_rows, low_rows = slice(0, half), slice(half, tokens)

    def project(rows, r):
        return jnp.dot(att[rows, :], w_buf[r], preferred_element_type=F32)

    opp_p = remote(opp.at[top_rows, :], relay_p, xs_sem.at[0], xr_sem.at[0], x_p)
    opp_m = remote(opp.at[low_rows, :], relay_m, xs_sem.at[1], xr_sem.at[1], x_m)
    plain_p = remote(to_p.at[low_rows, :], from_m.at[low_rows, :], xs_sem.at[2], xr_sem.at[2], x_p)
    plain_m = remote(to_m.at[top_rows, :], from_p.at[top_rows, :], xs_sem.at[3], xr_sem.at[3], x_m)
    sum_p = remote(to_p.at[top_rows, :], from_m.at[top_rows, :], xs_sem.at[4], xr_sem.at[4], x_p)
    sum_m = remote(to_m.at[low_rows, :], from_p.at[low_rows, :], xs_sem.at[5], xr_sem.at[5], x_m)

    opp[top_rows, :] = project(top_rows, 2).astype(BF16)
    opp_p.start()
    opp[low_rows, :] = project(low_rows, 2).astype(BF16)
    opp_m.start()
    to_p[low_rows, :] = project(low_rows, 1).astype(BF16)
    plain_p.start()
    to_m[top_rows, :] = project(top_rows, 3).astype(BF16)
    plain_m.start()
    mine_p = project(top_rows, 1)
    opp_p.wait_recv()
    to_p[top_rows, :] = (mine_p + relay_p[...].astype(F32)).astype(BF16)
    sum_p.start()
    mine_m = project(low_rows, 3)
    opp_m.wait_recv()
    to_m[low_rows, :] = (mine_m + relay_m[...].astype(F32)).astype(BF16)
    sum_m.start()
    own_top = project(top_rows, 0)
    own_low = project(low_rows, 0)
    plain_p.wait_recv()
    plain_m.wait_recv()
    sum_p.wait_recv()
    o_ref[top_rows, :] = (own_top + from_m[top_rows, :].astype(F32)
                          + from_p[top_rows, :].astype(F32)).astype(BF16)
    sum_m.wait_recv()
    o_ref[low_rows, :] = (own_low + from_m[low_rows, :].astype(F32)
                          + from_p[low_rows, :].astype(F32)).astype(BF16)
    for copy in (opp_p, opp_m, plain_p, plain_m, sum_p, sum_m):
        copy.wait_send()
    @pl.when(place < n_ctx - 1)
    def _():
        for which in range(parts):
            own_hop(which).wait_send()

    def settle(step, _):
        @pl.when(onward(step))
        def _():
            for which in range(parts):
                hop(which, step).wait_send()
        return 0

    lax.fori_loop(1, hops, settle, 0)
    if detour:
        @pl.when(((col == 9) | (col == 10)) & (row < n_row - 1))
        def _():
            for which in range(parts):
                leave(which, 5).wait_send()

        @pl.when(((col == 5) | (col == 6) | (col == 1)) & (row > 0))
        def _():
            for which in range(parts):
                pass_last(which).wait_send()


def solution(mesh):
    n_ctx, n_head = mesh.shape["ctx"], mesh.shape["head"]
    n_x = n_head // 2

    def body(queries, keys, values, segment_ids, out_weight):
        tokens, width = queries.shape
        heads = width // HEAD_DIM
        hops = min(-(-(DOC_MAX - 1) // tokens), n_ctx - 1)
        half = tokens // 2
        parts = 1 + 2 * PIECES
        any_space = pl.BlockSpec(memory_space=pl.ANY)
        dma = pltpu.SemaphoreType.DMA
        return pl.pallas_call(
            functools.partial(kernel, hops, n_ctx, n_x),
            out_shape=jax.ShapeDtypeStruct((tokens, width), BF16),
            in_specs=[any_space] * 5,
            out_specs=pl.BlockSpec(memory_space=pltpu.VMEM),
            scratch_shapes=[
                pltpu.VMEM((tokens, width), BF16),
                pltpu.VMEM((tokens, HEAD_DIM), BF16),
                pltpu.VMEM((tokens, HEAD_DIM), BF16),
                pltpu.VMEM((1, tokens), jnp.int32),
                pltpu.VMEM((hops, tokens, HEAD_DIM), BF16),
                pltpu.VMEM((hops, tokens, HEAD_DIM), BF16),
                pltpu.VMEM((hops, 1, tokens), jnp.int32),
                pltpu.VMEM((n_x, 2 * width, width), BF16),
                pltpu.VMEM((tokens, 2 * width), BF16),
                pltpu.VMEM((heads, tokens, 2 * HEAD_DIM), F32),
                pltpu.VMEM((heads, tokens, HEAD_DIM), F32),
                pltpu.VMEM((tokens, width), BF16),
                pltpu.VMEM((tokens, width), BF16),
                pltpu.VMEM((tokens, width), BF16),
                pltpu.VMEM((half, width), BF16),
                pltpu.VMEM((half, width), BF16),
                pltpu.VMEM((tokens, width), BF16),
                pltpu.VMEM((tokens, width), BF16),
                pltpu.VMEM((1, tokens), jnp.int32),
                pltpu.VMEM((tokens, HEAD_DIM), BF16),
                pltpu.VMEM((tokens, HEAD_DIM), BF16),
                pltpu.VMEM((heads, tokens, tokens), BF16),
                pltpu.VMEM((heads, tokens, HEAD_DIM), F32),
                dma((4,)),
                dma((n_x,)), dma((n_x,)), dma((n_x,)),
                dma((hops, parts)), dma((hops, parts)),
                dma((heads,)), dma((heads,)),
                dma((6,)), dma((6,)),
                dma((parts,)), dma((parts,)), dma((parts,)),
            ],
            compiler_params=pltpu.CompilerParams(collective_id=0, has_side_effects=True),
        )(queries, keys, values, segment_ids.reshape(1, tokens), out_weight)

    in_specs = (P("ctx", "head"), P("ctx", "head"), P("ctx", "head"), P("ctx"), P("head", None))
    return jax.shard_map(body, mesh=mesh, in_specs=in_specs, out_specs=P("ctx", "head"), check_vma=False)
```

```python
import functools
import math

import jax
import jax.numpy as jnp
from jax import lax
from jax.experimental import pallas as pl
from jax.experimental.pallas import tpu as pltpu
from jax.sharding import PartitionSpec as P

HEAD_DIM = 128
DOC_MAX = 1792
RING = 16
PIECES = 2
MESH = pl.DeviceIdType.MESH
NEG = -1e30
F32 = jnp.float32
BF16 = jnp.bfloat16


def kernel(hops, n_ctx, n_x, q_hbm, k_hbm, v_hbm, s_hbm, w_hbm, o_ref, from_m, from_p,
           q_own, k_own, v_own, s_own, kbuf, vbuf, sbuf, w_buf, att, acc, top,
           opp, to_p, to_m, relay_p, relay_m, own_sum,
           via_s, via_k, via_v, wts, fade,
           own_sem, wl_sem, ws_sem, wr_sem, hs_sem, hr_sem, as_sem, ar_sem, xs_sem, xr_sem,
           ds_sem, dr_sem, es_sem):
    tokens, width = q_own.shape
    heads = width // HEAD_DIM
    half = tokens // 2
    place = lax.axis_index("ctx")
    head = lax.axis_index("head")
    x, core = head // 2, head % 2
    nxt, prv = lax.rem(place + 1, n_ctx), lax.rem(place + n_ctx - 1, n_ctx)
    n_row = max(n_ctx // RING, 1)
    row, col = place // RING, lax.rem(place, RING)
    detour = hops == 7 and n_ctx % RING == 0 and n_row > 1

    def spot(turns, where):
        return (lax.rem(row + turns + n_row, n_row) * RING + where, head)

    partner = (place, x * 2 + (1 - core))
    x_p = (place, lax.rem(x + 1, n_x) * 2 + core)
    x_m = (place, lax.rem(x + n_x - 1, n_x) * 2 + core)
    c = math.log2(math.e) / math.sqrt(HEAD_DIM)

    def remote(src, dst, send, recv, device):
        return pltpu.make_async_remote_copy(
            src_ref=src, dst_ref=dst, send_sem=send, recv_sem=recv,
            device_id=device, device_id_type=MESH)

    local = [pltpu.make_async_copy(src, dst, own_sem.at[i]) for i, (src, dst) in enumerate(
        [(s_hbm, s_own), (k_hbm, k_own), (q_hbm, q_own), (v_hbm, v_own)])]
    for copy in local:
        copy.start()

    barrier = pltpu.get_barrier_semaphore()

    def greet(device):
        pl.semaphore_signal(barrier, inc=1, device_id=device, device_id_type=MESH)

    for device in ((prv, head), partner, x_p, x_m):
        greet(device)
    if detour:
        for where, sources in ((5, ((-1, 9),)), (6, ((-1, 10),)), (0, ((0, 5), (0, 1))), (1, ((0, 6),))):
            @pl.when(col == where)
            def _():
                for source in sources:
                    greet(spot(*source))
    if detour:
        further = (col == 9) | (col == 10) | (col == 5) | (col == 6) | (col == 1)
        pl.semaphore_wait(barrier, jnp.where(further, 5, 4))
    else:
        pl.semaphore_wait(barrier, 4)

    piece = tokens // PIECES
    parts = 1 + 2 * PIECES

    def part(refs, which, *slot):
        if which == 0:
            return refs[0].at[slot] if slot else refs[0]
        at = (which - 1) % PIECES * piece
        return refs[1 + (which - 1) // PIECES].at[(*slot, slice(at, at + piece), slice(None))]

    given, slots, via = (s_hbm, k_hbm, v_hbm), (sbuf, kbuf, vbuf), (via_s, via_k, via_v)

    def own_hop(which):
        return remote(part(given, which), part(slots, which, 0), hs_sem.at[0, which],
                      hr_sem.at[0, which], (nxt, head))

    def hop(which, step):
        return remote(part(slots, which, step - 1), part(slots, which, step), hs_sem.at[step, which],
                      hr_sem.at[step, which], (nxt, head))

    def arrived(which, step):
        return remote(part(slots, which, step), part(slots, which, step), hs_sem.at[step, which],
                      hr_sem.at[step, which], (nxt, head))

    def leave(which, where):
        return remote(part(given, which), part(via, which), ds_sem.at[which], dr_sem.at[which],
                      spot(1, where))

    def pass_on(which, where):
        return remote(part(via, which), part(slots, which, 6), es_sem.at[which], hr_sem.at[6, which],
                      spot(0, where))

    def pass_last(which):
        return remote(part(slots, which, 6), part(slots, which, 5), es_sem.at[which],
                      hr_sem.at[5, which], spot(0, 0))

    @pl.when(place < n_ctx - 1)
    def _():
        for which in range(parts):
            own_hop(which).start()

    if detour:
        for here, where in ((9, 5), (10, 6)):
            @pl.when((col == here) & (row < n_row - 1))
            def _():
                for which in range(parts):
                    leave(which, where).start()

    def w_local(r):
        col = pl.multiple_of((lax.rem(x + r, n_x) * 2 + core) * width, width)
        return pltpu.make_async_copy(
            w_hbm.at[:, pl.ds(col, width)], w_buf.at[r, 0:width, :], wl_sem.at[r])

    def w_remote(r):
        col = pl.multiple_of((lax.rem(x + r, n_x) * 2 + (1 - core)) * width, width)
        return remote(w_hbm.at[:, pl.ds(col, width)], w_buf.at[r, width:2 * width, :],
                      ws_sem.at[r], wr_sem.at[r], partner)

    for r in range(n_x):
        w_local(r).start()
        w_remote(r).start()

    for copy in local:
        copy.wait()

    ones = jnp.ones((tokens, HEAD_DIM), BF16)
    k_iota = lax.broadcasted_iota(jnp.int32, (tokens, tokens), 1)
    q_iota = lax.broadcasted_iota(jnp.int32, (tokens, tokens), 0)
    seg_row = s_own[...].astype(F32)
    first = jnp.min(seg_row, axis=1, keepdims=True)
    count_own = jnp.sum(jnp.where(seg_row == first, 1.0, 0.0), axis=1, keepdims=True).astype(jnp.int32)

    def scores(h, keys):
        return lax.dot_general(q_own[:, h * HEAD_DIM:(h + 1) * HEAD_DIM], keys,
                               (((1,), (1,)), ((), ())), preferred_element_type=F32)

    def blank(step, _):
        kbuf[step] = jnp.zeros((tokens, HEAD_DIM), BF16)
        vbuf[step] = jnp.zeros((tokens, HEAD_DIM), BF16)
        sbuf[step] = jnp.full((1, tokens), -1, jnp.int32)
        return 0

    lax.fori_loop(jnp.minimum(place, hops), hops, blank, 0)

    seg_col = jnp.transpose(jnp.broadcast_to(seg_row, (HEAD_DIM, tokens)))
    seg_col = jnp.concatenate([seg_col] * (tokens // HEAD_DIM), axis=1)
    visible = (seg_col == seg_row) & (k_iota <= q_iota)
    keys = k_own[...]
    v_ext = jnp.concatenate([v_own[...], ones], axis=1)
    for h in range(heads):
        s = jnp.where(visible, scores(h, keys), NEG)
        m = jnp.max(s, axis=1, keepdims=True)
        p = jnp.exp2((s - m) * c)
        acc[h] = jnp.dot(p.astype(BF16), v_ext, preferred_element_type=F32)
        top[h] = jnp.broadcast_to(m, (tokens, HEAD_DIM))

    def weigh(step, which_heads):
        ids = sbuf[step].astype(F32)
        count = jnp.sum(jnp.where(ids == first, 1.0, 0.0), axis=1, keepdims=True).astype(jnp.int32)
        count = jnp.where(place > step, count, 0)
        start = jnp.where(q_iota[:, 0:1] < count_own, tokens - count, tokens)
        keys = kbuf[step]
        for h in which_heads:
            s = jnp.where(k_iota >= start, scores(h, keys), NEG)
            m_old = top[h][:, 0:1]
            m = jnp.maximum(m_old, jnp.max(s, axis=1, keepdims=True))
            wts[h] = jnp.exp2((s - m) * c).astype(BF16)
            fade[h] = jnp.broadcast_to(jnp.exp2((m_old - m) * c), (tokens, HEAD_DIM))
            top[h] = jnp.broadcast_to(m, (tokens, HEAD_DIM))

    def gather(step, h):
        v_ext = jnp.concatenate([vbuf[step], ones], axis=1)
        return acc[h] * fade[h][:, 0:1] + jnp.dot(wts[h], v_ext, preferred_element_type=F32)

    def gather_all(step, which_heads):
        for h in which_heads:
            acc[h] = gather(step, h)

    def onward(step):
        going = (place >= step) & (place < n_ctx - 1)
        if detour:
            going &= jnp.logical_not(((col == RING - 1) & (step >= 5)) | ((col == 0) & (step == 6)))
        return going

    lower, upper = range(heads // 2), range(heads // 2, heads)

    def turn(step, after):
        for which in range(parts):
            @pl.when(place >= step)
            def _():
                arrived(which, step - 1).wait_recv()

            @pl.when(onward(step))
            def _():
                hop(which, step).start()
            after(which)
        if detour:
            for here, where in ((5, 0), (6, 1)):
                @pl.when((step == 4) & (col == here) & (row > 0))
                def _():
                    for which in range(parts):
                        leave(which, where).wait_recv()
                        pass_on(which, where).start()

            @pl.when((step == 4) & (col == 1) & (row > 0))
            def _():
                for which in range(parts):
                    arrived(which, 6).wait_recv()
                    pass_last(which).start()

    def first_turn(which):
        if which == PIECES + 1:
            weigh(0, lower)
        if which == parts - 1:
            weigh(0, upper)

    turn(1, first_turn)

    def later(step, _):
        def after(which):
            if which == 1:
                gather_all(step - 2, lower)
            if which == PIECES:
                gather_all(step - 2, upper)
            if which == PIECES + 1:
                weigh(step - 1, lower)
            if which == parts - 1:
                weigh(step - 1, upper)

        turn(step, after)
        return 0

    lax.fori_loop(2, hops, later, 0)
    waits = place >= hops
    if detour:
        waits &= col != 1
    if hops > 1:
        gather_all(hops - 2, range(heads))
    for wanted in (range(0, PIECES + 1), range(PIECES + 1, parts)):
        @pl.when(waits)
        def _():
            for which in wanted:
                arrived(which, hops - 1).wait_recv()
        if 0 in wanted and hops > 1:
            weigh(hops - 1, range(heads))

    def give(h):
        mine = att.at[:, h * HEAD_DIM:(h + 1) * HEAD_DIM]
        theirs = att.at[:, width + h * HEAD_DIM:width + (h + 1) * HEAD_DIM]
        return remote(mine, theirs, as_sem.at[h], ar_sem.at[h], partner)

    def finish(h, done):
        att[:, h * HEAD_DIM:(h + 1) * HEAD_DIM] = (
            done[:, :HEAD_DIM] / done[:, HEAD_DIM:]).astype(BF16)
        give(h).start()

    for h in range(heads):
        finish(h, gather(hops - 1, h))

    for r in range(n_x):
        w_local(r).wait()
        w_remote(r).wait()
    for h in range(heads):
        give(h).wait()

    top_rows, low_rows = slice(0, half), slice(half, tokens)

    def project(rows, r):
        return jnp.dot(att[rows, :], w_buf[r], preferred_element_type=F32)

    opp_p = remote(opp.at[top_rows, :], relay_p, xs_sem.at[0], xr_sem.at[0], x_p)
    opp_m = remote(opp.at[low_rows, :], relay_m, xs_sem.at[1], xr_sem.at[1], x_m)
    plain_p = remote(to_p.at[low_rows, :], from_m.at[low_rows, :], xs_sem.at[2], xr_sem.at[2], x_p)
    plain_m = remote(to_m.at[top_rows, :], from_p.at[top_rows, :], xs_sem.at[3], xr_sem.at[3], x_m)
    sum_p = remote(to_p.at[top_rows, :], from_m.at[top_rows, :], xs_sem.at[4], xr_sem.at[4], x_p)
    sum_m = remote(to_m.at[low_rows, :], from_p.at[low_rows, :], xs_sem.at[5], xr_sem.at[5], x_m)

    opp[top_rows, :] = project(top_rows, 2).astype(BF16)
    opp_p.start()
    opp[low_rows, :] = project(low_rows, 2).astype(BF16)
    opp_m.start()
    to_p[low_rows, :] = project(low_rows, 1).astype(BF16)
    plain_p.start()
    to_m[top_rows, :] = project(top_rows, 3).astype(BF16)
    plain_m.start()
    mine_p = project(top_rows, 1)
    opp_p.wait_recv()
    to_p[top_rows, :] = (mine_p + relay_p[...].astype(F32)).astype(BF16)
    sum_p.start()
    mine_m = project(low_rows, 3)
    opp_m.wait_recv()
    to_m[low_rows, :] = (mine_m + relay_m[...].astype(F32)).astype(BF16)
    sum_m.start()
    own_out = pltpu.make_async_copy(own_sum, o_ref, own_sem.at[0])
    own_sum[top_rows, :] = project(top_rows, 0)
    own_sum[low_rows, :] = project(low_rows, 0)
    own_out.start()
    plain_p.wait_recv()
    plain_m.wait_recv()
    sum_p.wait_recv()
    sum_m.wait_recv()
    own_out.wait()
    for copy in (opp_p, opp_m, plain_p, plain_m, sum_p, sum_m):
        copy.wait_send()
    @pl.when(place < n_ctx - 1)
    def _():
        for which in range(parts):
            own_hop(which).wait_send()

    def settle(step, _):
        @pl.when(onward(step))
        def _():
            for which in range(parts):
                hop(which, step).wait_send()
        return 0

    lax.fori_loop(1, hops, settle, 0)
    if detour:
        @pl.when(((col == 9) | (col == 10)) & (row < n_row - 1))
        def _():
            for which in range(parts):
                leave(which, 5).wait_send()

        @pl.when(((col == 5) | (col == 6) | (col == 1)) & (row > 0))
        def _():
            for which in range(parts):
                pass_last(which).wait_send()


def solution(mesh):
    n_ctx, n_head = mesh.shape["ctx"], mesh.shape["head"]
    n_x = n_head // 2

    def body(queries, keys, values, segment_ids, out_weight):
        tokens, width = queries.shape
        heads = width // HEAD_DIM
        hops = min(-(-(DOC_MAX - 1) // tokens), n_ctx - 1)
        half = tokens // 2
        parts = 1 + 2 * PIECES
        any_space = pl.BlockSpec(memory_space=pl.ANY)
        dma = pltpu.SemaphoreType.DMA
        own, from_m, from_p = pl.pallas_call(
            functools.partial(kernel, hops, n_ctx, n_x),
            out_shape=[jax.ShapeDtypeStruct((tokens, width), kind) for kind in (F32, BF16, BF16)],
            in_specs=[any_space] * 5,
            out_specs=[any_space] * 3,
            scratch_shapes=[
                pltpu.VMEM((tokens, width), BF16),
                pltpu.VMEM((tokens, HEAD_DIM), BF16),
                pltpu.VMEM((tokens, HEAD_DIM), BF16),
                pltpu.VMEM((1, tokens), jnp.int32),
                pltpu.VMEM((hops, tokens, HEAD_DIM), BF16),
                pltpu.VMEM((hops, tokens, HEAD_DIM), BF16),
                pltpu.VMEM((hops, 1, tokens), jnp.int32),
                pltpu.VMEM((n_x, 2 * width, width), BF16),
                pltpu.VMEM((tokens, 2 * width), BF16),
                pltpu.VMEM((heads, tokens, 2 * HEAD_DIM), F32),
                pltpu.VMEM((heads, tokens, HEAD_DIM), F32),
                pltpu.VMEM((tokens, width), BF16),
                pltpu.VMEM((tokens, width), BF16),
                pltpu.VMEM((tokens, width), BF16),
                pltpu.VMEM((half, width), BF16),
                pltpu.VMEM((half, width), BF16),
                pltpu.VMEM((tokens, width), F32),
                pltpu.VMEM((1, tokens), jnp.int32),
                pltpu.VMEM((tokens, HEAD_DIM), BF16),
                pltpu.VMEM((tokens, HEAD_DIM), BF16),
                pltpu.VMEM((heads, tokens, tokens), BF16),
                pltpu.VMEM((heads, tokens, HEAD_DIM), F32),
                dma((4,)),
                dma((n_x,)), dma((n_x,)), dma((n_x,)),
                dma((hops, parts)), dma((hops, parts)),
                dma((heads,)), dma((heads,)),
                dma((6,)), dma((6,)),
                dma((parts,)), dma((parts,)), dma((parts,)),
            ],
            compiler_params=pltpu.CompilerParams(collective_id=0, has_side_effects=True),
        )(queries, keys, values, segment_ids.reshape(1, tokens), out_weight)
        return (own + from_m.astype(F32) + from_p.astype(F32)).astype(BF16)

    in_specs = (P("ctx", "head"), P("ctx", "head"), P("ctx", "head"), P("ctx"), P("head", None))
    return jax.shard_map(body, mesh=mesh, in_specs=in_specs, out_specs=P("ctx", "head"), check_vma=False)
```

```python
import functools
import math

import jax
import jax.numpy as jnp
from jax import lax
from jax.experimental import pallas as pl
from jax.experimental.pallas import tpu as pltpu
from jax.sharding import PartitionSpec as P

HEAD_DIM = 128
DOC_MAX = 1792
RING = 16
PIECES = 4
MESH = pl.DeviceIdType.MESH
NEG = -1e30
F32 = jnp.float32
BF16 = jnp.bfloat16


def kernel(hops, n_ctx, n_x, q_hbm, k_hbm, v_hbm, s_hbm, w_hbm, o_ref, late,
           q_own, k_own, v_own, s_own, kbuf, vbuf, sbuf, w_buf, att, acc, top,
           opp, to_p, to_m, relay_p, relay_m, early_p, early_m, own_sum,
           via_s, via_k, via_v, wts, fade,
           own_sem, wl_sem, ws_sem, wr_sem, hs_sem, hr_sem, as_sem, ar_sem, xs_sem, xr_sem,
           ds_sem, dr_sem, es_sem):
    tokens, width = q_own.shape
    heads = width // HEAD_DIM
    half = tokens // 2
    place = lax.axis_index("ctx")
    head = lax.axis_index("head")
    x, core = head // 2, head % 2
    nxt, prv = lax.rem(place + 1, n_ctx), lax.rem(place + n_ctx - 1, n_ctx)
    n_row = max(n_ctx // RING, 1)
    row, col = place // RING, lax.rem(place, RING)
    detour = hops == 7 and n_ctx % RING == 0 and n_row > 1

    def spot(turns, where):
        return (lax.rem(row + turns + n_row, n_row) * RING + where, head)

    partner = (place, x * 2 + (1 - core))
    x_p = (place, lax.rem(x + 1, n_x) * 2 + core)
    x_m = (place, lax.rem(x + n_x - 1, n_x) * 2 + core)
    c = math.log2(math.e) / math.sqrt(HEAD_DIM)

    def remote(src, dst, send, recv, device):
        return pltpu.make_async_remote_copy(
            src_ref=src, dst_ref=dst, send_sem=send, recv_sem=recv,
            device_id=device, device_id_type=MESH)

    local = [pltpu.make_async_copy(src, dst, own_sem.at[i]) for i, (src, dst) in enumerate(
        [(s_hbm, s_own), (k_hbm, k_own), (q_hbm, q_own), (v_hbm, v_own)])]
    for copy in local:
        copy.start()

    barrier = pltpu.get_barrier_semaphore()

    def greet(device):
        pl.semaphore_signal(barrier, inc=1, device_id=device, device_id_type=MESH)

    for device in ((prv, head), partner, x_p, x_m):
        greet(device)
    if detour:
        for where, sources in ((5, ((-1, 9),)), (6, ((-1, 10),)), (0, ((0, 5), (0, 1))), (1, ((0, 6),))):
            @pl.when(col == where)
            def _():
                for source in sources:
                    greet(spot(*source))
    if detour:
        further = (col == 9) | (col == 10) | (col == 5) | (col == 6) | (col == 1)
        pl.semaphore_wait(barrier, jnp.where(further, 5, 4))
    else:
        pl.semaphore_wait(barrier, 4)

    piece = tokens // PIECES
    parts = 1 + 2 * PIECES

    def part(refs, which, *slot):
        if which == 0:
            return refs[0].at[slot] if slot else refs[0]
        at = (which - 1) % PIECES * piece
        return refs[1 + (which - 1) // PIECES].at[(*slot, slice(at, at + piece), slice(None))]

    given, slots, via = (s_hbm, k_hbm, v_hbm), (sbuf, kbuf, vbuf), (via_s, via_k, via_v)

    def own_hop(which):
        return remote(part(given, which), part(slots, which, 0), hs_sem.at[0, which],
                      hr_sem.at[0, which], (nxt, head))

    def hop(which, step):
        return remote(part(slots, which, step - 1), part(slots, which, step), hs_sem.at[step, which],
                      hr_sem.at[step, which], (nxt, head))

    def arrived(which, step):
        return remote(part(slots, which, step), part(slots, which, step), hs_sem.at[step, which],
                      hr_sem.at[step, which], (nxt, head))

    def leave(which, where):
        return remote(part(given, which), part(via, which), ds_sem.at[which], dr_sem.at[which],
                      spot(1, where))

    def pass_on(which, where):
        return remote(part(via, which), part(slots, which, 6), es_sem.at[which], hr_sem.at[6, which],
                      spot(0, where))

    def pass_last(which):
        return remote(part(slots, which, 6), part(slots, which, 5), es_sem.at[which],
                      hr_sem.at[5, which], spot(0, 0))

    @pl.when(place < n_ctx - 1)
    def _():
        for which in range(parts):
            own_hop(which).start()

    if detour:
        for here, where in ((9, 5), (10, 6)):
            @pl.when((col == here) & (row < n_row - 1))
            def _():
                for which in range(parts):
                    leave(which, where).start()

    def w_local(r):
        col = pl.multiple_of((lax.rem(x + r, n_x) * 2 + core) * width, width)
        return pltpu.make_async_copy(
            w_hbm.at[:, pl.ds(col, width)], w_buf.at[r, 0:width, :], wl_sem.at[r])

    def w_remote(r):
        col = pl.multiple_of((lax.rem(x + r, n_x) * 2 + (1 - core)) * width, width)
        return remote(w_hbm.at[:, pl.ds(col, width)], w_buf.at[r, width:2 * width, :],
                      ws_sem.at[r], wr_sem.at[r], partner)

    for r in range(n_x):
        w_local(r).start()
        w_remote(r).start()

    for copy in local:
        copy.wait()

    ones = jnp.ones((tokens, HEAD_DIM), BF16)
    k_iota = lax.broadcasted_iota(jnp.int32, (tokens, tokens), 1)
    q_iota = lax.broadcasted_iota(jnp.int32, (tokens, tokens), 0)
    seg_row = s_own[...].astype(F32)
    first = jnp.min(seg_row, axis=1, keepdims=True)
    count_own = jnp.sum(jnp.where(seg_row == first, 1.0, 0.0), axis=1, keepdims=True).astype(jnp.int32)

    def scores(h, keys):
        return lax.dot_general(q_own[:, h * HEAD_DIM:(h + 1) * HEAD_DIM], keys,
                               (((1,), (1,)), ((), ())), preferred_element_type=F32)

    def blank(step, _):
        kbuf[step] = jnp.zeros((tokens, HEAD_DIM), BF16)
        vbuf[step] = jnp.zeros((tokens, HEAD_DIM), BF16)
        sbuf[step] = jnp.full((1, tokens), -1, jnp.int32)
        return 0

    lax.fori_loop(jnp.minimum(place, hops), hops, blank, 0)

    seg_col = jnp.transpose(jnp.broadcast_to(seg_row, (HEAD_DIM, tokens)))
    seg_col = jnp.concatenate([seg_col] * (tokens // HEAD_DIM), axis=1)
    visible = (seg_col == seg_row) & (k_iota <= q_iota)
    keys = k_own[...]
    v_ext = jnp.concatenate([v_own[...], ones], axis=1)
    for h in range(heads):
        s = jnp.where(visible, scores(h, keys), NEG)
        m = jnp.max(s, axis=1, keepdims=True)
        p = jnp.exp2((s - m) * c)
        acc[h] = jnp.dot(p.astype(BF16), v_ext, preferred_element_type=F32)
        top[h] = jnp.broadcast_to(m, (tokens, HEAD_DIM))

    def weigh(step, which_heads):
        ids = sbuf[step].astype(F32)
        count = jnp.sum(jnp.where(ids == first, 1.0, 0.0), axis=1, keepdims=True).astype(jnp.int32)
        count = jnp.where(place > step, count, 0)
        start = jnp.where(q_iota[:, 0:1] < count_own, tokens - count, tokens)
        keys = kbuf[step]
        for h in which_heads:
            s = jnp.where(k_iota >= start, scores(h, keys), NEG)
            m_old = top[h][:, 0:1]
            m = jnp.maximum(m_old, jnp.max(s, axis=1, keepdims=True))
            wts[h] = jnp.exp2((s - m) * c).astype(BF16)
            fade[h] = jnp.broadcast_to(jnp.exp2((m_old - m) * c), (tokens, HEAD_DIM))
            top[h] = jnp.broadcast_to(m, (tokens, HEAD_DIM))

    def gather(step, h):
        v_ext = jnp.concatenate([vbuf[step], ones], axis=1)
        return acc[h] * fade[h][:, 0:1] + jnp.dot(wts[h], v_ext, preferred_element_type=F32)

    def gather_all(step, which_heads):
        for h in which_heads:
            acc[h] = gather(step, h)

    def onward(step):
        going = (place >= step) & (place < n_ctx - 1) & (step < hops)
        if detour:
            going &= jnp.logical_not(((col == RING - 1) & (step >= 5)) | ((col == 0) & (step == 6)))
        return going

    lower, upper = range(heads // 2), range(heads // 2, heads)

    def order(turns):
        if not detour:
            return turns
        return jnp.where((col == 0) & (turns >= 4), jnp.where(turns == 4, 6, turns - 1), turns)

    def due(slot):
        here = place > slot
        if detour:
            here &= jnp.logical_not((col == 1) & (slot == 6))
        return here

    def turn(step, after):
        slot = order(step - 1)
        for which in range(parts):
            @pl.when(due(slot))
            def _():
                arrived(which, slot).wait_recv()

            @pl.when(onward(slot + 1))
            def _():
                hop(which, slot + 1).start()
            after(which)
        if detour:
            for here, where in ((5, 0), (6, 1)):
                @pl.when((step == 4) & (col == here) & (row > 0))
                def _():
                    for which in range(parts):
                        leave(which, where).wait_recv()
                        pass_on(which, where).start()

            @pl.when((step == 4) & (col == 1) & (row > 0))
            def _():
                for which in range(parts):
                    arrived(which, 6).wait_recv()
                    pass_last(which).start()

    def first_turn(which):
        if which == PIECES + 1:
            weigh(0, lower)
        if which == parts - 1:
            weigh(0, upper)

    turn(1, first_turn)

    def later(step, _):
        def after(which):
            if which == 1:
                gather_all(order(step - 2), lower)
            if which == PIECES:
                gather_all(order(step - 2), upper)
            if which == PIECES + 1:
                weigh(order(step - 1), lower)
            if which == parts - 1:
                weigh(order(step - 1), upper)

        turn(step, after)
        return 0

    lax.fori_loop(2, hops, later, 0)
    if hops > 1:
        gather_all(order(hops - 2), range(heads))
    end = order(hops - 1)
    for wanted in (range(0, PIECES + 1), range(PIECES + 1, parts)):
        @pl.when(due(end))
        def _():
            for which in wanted:
                arrived(which, end).wait_recv()
        if 0 in wanted and hops > 1:
            weigh(end, range(heads))

    def give(h):
        mine = att.at[:, h * HEAD_DIM:(h + 1) * HEAD_DIM]
        theirs = att.at[:, width + h * HEAD_DIM:width + (h + 1) * HEAD_DIM]
        return remote(mine, theirs, as_sem.at[h], ar_sem.at[h], partner)

    def finish(h, done):
        att[:, h * HEAD_DIM:(h + 1) * HEAD_DIM] = (
            done[:, :HEAD_DIM] / done[:, HEAD_DIM:]).astype(BF16)
        give(h).start()

    for h in range(heads):
        finish(h, gather(end, h))

    for r in range(n_x):
        w_local(r).wait()
        w_remote(r).wait()

    top_rows, low_rows = slice(0, half), slice(half, tokens)

    def share(rows, r, side):
        at = slice(side * width, (side + 1) * width)
        return jnp.dot(att[rows, at], w_buf[r, at, :], preferred_element_type=F32)

    opp_top, opp_low = share(top_rows, 2, 0), share(low_rows, 2, 0)
    for h in range(heads):
        give(h).wait()

    def project(rows, r):
        return jnp.dot(att[rows, :], w_buf[r], preferred_element_type=F32)

    opp_p = remote(opp.at[top_rows, :], relay_p, xs_sem.at[0], xr_sem.at[0], x_p)
    opp_m = remote(opp.at[low_rows, :], relay_m, xs_sem.at[1], xr_sem.at[1], x_m)
    plain_p = remote(to_p.at[low_rows, :], early_m, xs_sem.at[2], xr_sem.at[2], x_p)
    plain_m = remote(to_m.at[top_rows, :], early_p, xs_sem.at[3], xr_sem.at[3], x_m)
    sum_p = remote(to_p.at[top_rows, :], late.at[top_rows, :], xs_sem.at[4], xr_sem.at[4], x_p)
    sum_m = remote(to_m.at[low_rows, :], late.at[low_rows, :], xs_sem.at[5], xr_sem.at[5], x_m)

    opp[top_rows, :] = (opp_top + share(top_rows, 2, 1)).astype(BF16)
    opp_p.start()
    opp[low_rows, :] = (opp_low + share(low_rows, 2, 1)).astype(BF16)
    opp_m.start()
    to_p[low_rows, :] = project(low_rows, 1).astype(BF16)
    plain_p.start()
    to_m[top_rows, :] = project(top_rows, 3).astype(BF16)
    plain_m.start()
    mine_p = project(top_rows, 1)
    opp_p.wait_recv()
    to_p[top_rows, :] = (mine_p + relay_p[...].astype(F32)).astype(BF16)
    sum_p.start()
    mine_m = project(low_rows, 3)
    opp_m.wait_recv()
    to_m[low_rows, :] = (mine_m + relay_m[...].astype(F32)).astype(BF16)
    sum_m.start()
    own_out = pltpu.make_async_copy(own_sum, o_ref, own_sem.at[0])
    mine_top = project(top_rows, 0)
    mine_low = project(low_rows, 0)
    plain_m.wait_recv()
    own_sum[top_rows, :] = mine_top + early_p[...].astype(F32)
    plain_p.wait_recv()
    own_sum[low_rows, :] = mine_low + early_m[...].astype(F32)
    own_out.start()
    own_out.wait()
    sum_p.wait_recv()
    sum_m.wait_recv()
    for copy in (opp_p, opp_m, plain_p, plain_m, sum_p, sum_m):
        copy.wait_send()
    @pl.when(place < n_ctx - 1)
    def _():
        for which in range(parts):
            own_hop(which).wait_send()

    def settle(step, _):
        @pl.when(onward(step))
        def _():
            for which in range(parts):
                hop(which, step).wait_send()
        return 0

    lax.fori_loop(1, hops, settle, 0)
    if detour:
        @pl.when(((col == 9) | (col == 10)) & (row < n_row - 1))
        def _():
            for which in range(parts):
                leave(which, 5).wait_send()

        @pl.when(((col == 5) | (col == 6) | (col == 1)) & (row > 0))
        def _():
            for which in range(parts):
                pass_last(which).wait_send()


def solution(mesh):
    n_ctx, n_head = mesh.shape["ctx"], mesh.shape["head"]
    n_x = n_head // 2

    def body(queries, keys, values, segment_ids, out_weight):
        tokens, width = queries.shape
        heads = width // HEAD_DIM
        hops = min(-(-(DOC_MAX - 1) // tokens), n_ctx - 1)
        half = tokens // 2
        parts = 1 + 2 * PIECES
        any_space = pl.BlockSpec(memory_space=pl.ANY)
        dma = pltpu.SemaphoreType.DMA
        own, late = pl.pallas_call(
            functools.partial(kernel, hops, n_ctx, n_x),
            out_shape=[jax.ShapeDtypeStruct((tokens, width), kind) for kind in (F32, BF16)],
            in_specs=[any_space] * 5,
            out_specs=[any_space] * 2,
            scratch_shapes=[
                pltpu.VMEM((tokens, width), BF16),
                pltpu.VMEM((tokens, HEAD_DIM), BF16),
                pltpu.VMEM((tokens, HEAD_DIM), BF16),
                pltpu.VMEM((1, tokens), jnp.int32),
                pltpu.VMEM((hops, tokens, HEAD_DIM), BF16),
                pltpu.VMEM((hops, tokens, HEAD_DIM), BF16),
                pltpu.VMEM((hops, 1, tokens), jnp.int32),
                pltpu.VMEM((n_x, 2 * width, width), BF16),
                pltpu.VMEM((tokens, 2 * width), BF16),
                pltpu.VMEM((heads, tokens, 2 * HEAD_DIM), F32),
                pltpu.VMEM((heads, tokens, HEAD_DIM), F32),
                pltpu.VMEM((tokens, width), BF16),
                pltpu.VMEM((tokens, width), BF16),
                pltpu.VMEM((tokens, width), BF16),
                pltpu.VMEM((half, width), BF16),
                pltpu.VMEM((half, width), BF16),
                pltpu.VMEM((half, width), BF16),
                pltpu.VMEM((half, width), BF16),
                pltpu.VMEM((tokens, width), F32),
                pltpu.VMEM((1, tokens), jnp.int32),
                pltpu.VMEM((tokens, HEAD_DIM), BF16),
                pltpu.VMEM((tokens, HEAD_DIM), BF16),
                pltpu.VMEM((heads, tokens, tokens), BF16),
                pltpu.VMEM((heads, tokens, HEAD_DIM), F32),
                dma((4,)),
                dma((n_x,)), dma((n_x,)), dma((n_x,)),
                dma((hops, parts)), dma((hops, parts)),
                dma((heads,)), dma((heads,)),
                dma((6,)), dma((6,)),
                dma((parts,)), dma((parts,)), dma((parts,)),
            ],
            compiler_params=pltpu.CompilerParams(collective_id=0, has_side_effects=True),
        )(queries, keys, values, segment_ids.reshape(1, tokens), out_weight)
        return (own + late.astype(F32)).astype(BF16)

    in_specs = (P("ctx", "head"), P("ctx", "head"), P("ctx", "head"), P("ctx"), P("head", None))
    return jax.shard_map(body, mesh=mesh, in_specs=in_specs, out_specs=P("ctx", "head"), check_vma=False)
```

```python
import functools
import math

import jax
import jax.numpy as jnp
from jax import lax
from jax.experimental import pallas as pl
from jax.experimental.pallas import tpu as pltpu
from jax.sharding import PartitionSpec as P

HEAD_DIM = 128
DOC_MAX = 1792
RING = 16
PIECES = 2
MESH = pl.DeviceIdType.MESH
NEG = -1e30
F32 = jnp.float32
BF16 = jnp.bfloat16


def kernel(hops, n_ctx, n_x, q_hbm, k_hbm, v_hbm, s_hbm, w_hbm, o_ref, late,
           q_own, k_own, v_own, s_own, kbuf, vbuf, sbuf, w_buf, att, acc, top,
           opp, to_p, to_m, relay_p, relay_m, early_p, early_m, own_sum,
           via_s, via_k, via_v, wts, fade,
           own_sem, wl_sem, ws_sem, wr_sem, hs_sem, hr_sem, as_sem, ar_sem, xs_sem, xr_sem,
           ds_sem, dr_sem, es_sem):
    tokens, width = q_own.shape
    heads = width // HEAD_DIM
    half = tokens // 2
    place = lax.axis_index("ctx")
    head = lax.axis_index("head")
    x, core = head // 2, head % 2
    nxt, prv = lax.rem(place + 1, n_ctx), lax.rem(place + n_ctx - 1, n_ctx)
    n_row = max(n_ctx // RING, 1)
    row, col = place // RING, lax.rem(place, RING)
    detour = hops == 7 and n_ctx % RING == 0 and n_row > 1

    def spot(turns, where):
        return (lax.rem(row + turns + n_row, n_row) * RING + where, head)

    partner = (place, x * 2 + (1 - core))
    x_p = (place, lax.rem(x + 1, n_x) * 2 + core)
    x_m = (place, lax.rem(x + n_x - 1, n_x) * 2 + core)
    c = math.log2(math.e) / math.sqrt(HEAD_DIM)

    def remote(src, dst, send, recv, device):
        return pltpu.make_async_remote_copy(
            src_ref=src, dst_ref=dst, send_sem=send, recv_sem=recv,
            device_id=device, device_id_type=MESH)

    local = [pltpu.make_async_copy(src, dst, own_sem.at[i]) for i, (src, dst) in enumerate(
        [(s_hbm, s_own), (k_hbm, k_own), (q_hbm, q_own), (v_hbm, v_own)])]
    for copy in local:
        copy.start()

    barrier = pltpu.get_barrier_semaphore()

    def greet(device):
        pl.semaphore_signal(barrier, inc=1, device_id=device, device_id_type=MESH)

    for device in ((prv, head), partner, x_p, x_m):
        greet(device)
    if detour:
        for where, sources in ((5, ((-1, 9),)), (6, ((-1, 10),)), (0, ((0, 5), (0, 1))), (1, ((0, 6),))):
            @pl.when(col == where)
            def _():
                for source in sources:
                    greet(spot(*source))
    if detour:
        further = (col == 9) | (col == 10) | (col == 5) | (col == 6) | (col == 1)
        pl.semaphore_wait(barrier, jnp.where(further, 5, 4))
    else:
        pl.semaphore_wait(barrier, 4)

    piece = tokens // PIECES
    parts = 1 + 2 * PIECES

    def part(refs, which, *slot):
        if which == 0:
            return refs[0].at[slot] if slot else refs[0]
        at = (which - 1) % PIECES * piece
        return refs[1 + (which - 1) // PIECES].at[(*slot, slice(at, at + piece), slice(None))]

    given, slots, via = (s_hbm, k_hbm, v_hbm), (sbuf, kbuf, vbuf), (via_s, via_k, via_v)

    def own_hop(which):
        return remote(part(given, which), part(slots, which, 0), hs_sem.at[0, which],
                      hr_sem.at[0, which], (nxt, head))

    def hop(which, step):
        return remote(part(slots, which, step - 1), part(slots, which, step), hs_sem.at[step, which],
                      hr_sem.at[step, which], (nxt, head))

    def arrived(which, step):
        return remote(part(slots, which, step), part(slots, which, step), hs_sem.at[step, which],
                      hr_sem.at[step, which], (nxt, head))

    def leave(which, where):
        return remote(part(given, which), part(via, which), ds_sem.at[which], dr_sem.at[which],
                      spot(1, where))

    def pass_on(which, where):
        return remote(part(via, which), part(slots, which, 6), es_sem.at[which], hr_sem.at[6, which],
                      spot(0, where))

    def pass_last(which):
        return remote(part(slots, which, 6), part(slots, which, 5), es_sem.at[which],
                      hr_sem.at[5, which], spot(0, 0))

    @pl.when(place < n_ctx - 1)
    def _():
        for which in range(parts):
            own_hop(which).start()

    if detour:
        for here, where in ((9, 5), (10, 6)):
            @pl.when((col == here) & (row < n_row - 1))
            def _():
                for which in range(parts):
                    leave(which, where).start()

    def w_local(r):
        col = pl.multiple_of((lax.rem(x + r, n_x) * 2 + core) * width, width)
        return pltpu.make_async_copy(
            w_hbm.at[:, pl.ds(col, width)], w_buf.at[r, 0:width, :], wl_sem.at[r])

    def w_remote(r):
        col = pl.multiple_of((lax.rem(x + r, n_x) * 2 + (1 - core)) * width, width)
        return remote(w_hbm.at[:, pl.ds(col, width)], w_buf.at[r, width:2 * width, :],
                      ws_sem.at[r], wr_sem.at[r], partner)

    for r in range(n_x):
        w_local(r).start()
        w_remote(r).start()

    for copy in local:
        copy.wait()

    ones = jnp.ones((tokens, HEAD_DIM), BF16)
    k_iota = lax.broadcasted_iota(jnp.int32, (tokens, tokens), 1)
    q_iota = lax.broadcasted_iota(jnp.int32, (tokens, tokens), 0)
    seg_row = s_own[...].astype(F32)
    first = jnp.min(seg_row, axis=1, keepdims=True)
    count_own = jnp.sum(jnp.where(seg_row == first, 1.0, 0.0), axis=1, keepdims=True).astype(jnp.int32)

    def scores(h, keys):
        return lax.dot_general(q_own[:, h * HEAD_DIM:(h + 1) * HEAD_DIM], keys,
                               (((1,), (1,)), ((), ())), preferred_element_type=F32)

    def blank(step, _):
        kbuf[step] = jnp.zeros((tokens, HEAD_DIM), BF16)
        vbuf[step] = jnp.zeros((tokens, HEAD_DIM), BF16)
        sbuf[step] = jnp.full((1, tokens), -1, jnp.int32)
        return 0

    lax.fori_loop(jnp.minimum(place, hops), hops, blank, 0)

    seg_col = jnp.transpose(jnp.broadcast_to(seg_row, (HEAD_DIM, tokens)))
    seg_col = jnp.concatenate([seg_col] * (tokens // HEAD_DIM), axis=1)
    visible = (seg_col == seg_row) & (k_iota <= q_iota)
    keys = k_own[...]
    v_ext = jnp.concatenate([v_own[...], ones], axis=1)
    for h in range(heads):
        s = jnp.where(visible, scores(h, keys), NEG)
        m = jnp.max(s, axis=1, keepdims=True)
        p = jnp.exp2((s - m) * c)
        acc[h] = jnp.dot(p.astype(BF16), v_ext, preferred_element_type=F32)
        top[h] = jnp.broadcast_to(m, (tokens, HEAD_DIM))

    def weigh(step, which_heads):
        ids = sbuf[step].astype(F32)
        count = jnp.sum(jnp.where(ids == first, 1.0, 0.0), axis=1, keepdims=True).astype(jnp.int32)
        count = jnp.where(place > step, count, 0)
        start = jnp.where(q_iota[:, 0:1] < count_own, tokens - count, tokens)
        keys = kbuf[step]
        for h in which_heads:
            s = jnp.where(k_iota >= start, scores(h, keys), NEG)
            m_old = top[h][:, 0:1]
            m = jnp.maximum(m_old, jnp.max(s, axis=1, keepdims=True))
            wts[h] = jnp.exp2((s - m) * c).astype(BF16)
            fade[h] = jnp.broadcast_to(jnp.exp2((m_old - m) * c), (tokens, HEAD_DIM))
            top[h] = jnp.broadcast_to(m, (tokens, HEAD_DIM))

    def gather(step, h):
        v_ext = jnp.concatenate([vbuf[step], ones], axis=1)
        return acc[h] * fade[h][:, 0:1] + jnp.dot(wts[h], v_ext, preferred_element_type=F32)

    def gather_all(step, which_heads):
        for h in which_heads:
            acc[h] = gather(step, h)

    def onward(step):
        going = (place >= step) & (place < n_ctx - 1) & (step < hops)
        if detour:
            going &= jnp.logical_not(((col == RING - 1) & (step >= 5)) | ((col == 0) & (step == 6)))
        return going

    lower, upper = range(heads // 2), range(heads // 2, heads)

    def order(turns):
        if not detour:
            return turns
        return jnp.where((col == 0) & (turns >= 4), jnp.where(turns == 4, 6, turns - 1), turns)

    def due(slot):
        here = place > slot
        if detour:
            here &= jnp.logical_not((col == 1) & (slot == 6))
        return here

    def turn(step, after):
        slot = order(step - 1)
        for which in range(parts):
            @pl.when(due(slot))
            def _():
                arrived(which, slot).wait_recv()

            @pl.when(onward(slot + 1))
            def _():
                hop(which, slot + 1).start()
            after(which)
        if detour:
            for here, where in ((5, 0), (6, 1)):
                @pl.when((step == 4) & (col == here) & (row > 0))
                def _():
                    for which in range(parts):
                        leave(which, where).wait_recv()
                        pass_on(which, where).start()

            @pl.when((step == 4) & (col == 1) & (row > 0))
            def _():
                for which in range(parts):
                    arrived(which, 6).wait_recv()
                    pass_last(which).start()

    def first_turn(which):
        if which == PIECES + 1:
            weigh(0, lower)
        if which == parts - 1:
            weigh(0, upper)

    turn(1, first_turn)

    def later(step, _):
        def after(which):
            if which == 1:
                gather_all(order(step - 2), lower)
            if which == PIECES:
                gather_all(order(step - 2), upper)
            if which == PIECES + 1:
                weigh(order(step - 1), lower)
            if which == parts - 1:
                weigh(order(step - 1), upper)

        turn(step, after)
        return 0

    lax.fori_loop(2, hops, later, 0)
    if hops > 1:
        gather_all(order(hops - 2), range(heads))
    end = order(hops - 1)
    for wanted in (range(0, PIECES + 1), range(PIECES + 1, parts)):
        @pl.when(due(end))
        def _():
            for which in wanted:
                arrived(which, end).wait_recv()
        if 0 in wanted and hops > 1:
            weigh(end, range(heads))

    def give(h):
        mine = att.at[:, h * HEAD_DIM:(h + 1) * HEAD_DIM]
        theirs = att.at[:, width + h * HEAD_DIM:width + (h + 1) * HEAD_DIM]
        return remote(mine, theirs, as_sem.at[h], ar_sem.at[h], partner)

    def finish(h, done):
        att[:, h * HEAD_DIM:(h + 1) * HEAD_DIM] = (
            done[:, :HEAD_DIM] / done[:, HEAD_DIM:]).astype(BF16)
        give(h).start()

    for h in range(heads):
        finish(h, gather(end, h))

    for r in range(n_x):
        w_local(r).wait()
        w_remote(r).wait()

    top_rows, low_rows = slice(0, half), slice(half, tokens)

    def share(rows, r, side):
        at = slice(side * width, (side + 1) * width)
        return jnp.dot(att[rows, at], w_buf[r, at, :], preferred_element_type=F32)

    opp_top, opp_low = share(top_rows, 2, 0), share(low_rows, 2, 0)
    for h in range(heads):
        give(h).wait()

    def project(rows, r):
        return jnp.dot(att[rows, :], w_buf[r], preferred_element_type=F32)

    opp_p = remote(opp.at[top_rows, :], relay_p, xs_sem.at[0], xr_sem.at[0], x_p)
    opp_m = remote(opp.at[low_rows, :], relay_m, xs_sem.at[1], xr_sem.at[1], x_m)
    plain_p = remote(to_p.at[low_rows, :], early_m, xs_sem.at[2], xr_sem.at[2], x_p)
    plain_m = remote(to_m.at[top_rows, :], early_p, xs_sem.at[3], xr_sem.at[3], x_m)
    sum_p = remote(to_p.at[top_rows, :], late.at[top_rows, :], xs_sem.at[4], xr_sem.at[4], x_p)
    sum_m = remote(to_m.at[low_rows, :], late.at[low_rows, :], xs_sem.at[5], xr_sem.at[5], x_m)

    opp[top_rows, :] = (opp_top + share(top_rows, 2, 1)).astype(BF16)
    opp_p.start()
    opp[low_rows, :] = (opp_low + share(low_rows, 2, 1)).astype(BF16)
    opp_m.start()
    to_p[low_rows, :] = project(low_rows, 1).astype(BF16)
    plain_p.start()
    to_m[top_rows, :] = project(top_rows, 3).astype(BF16)
    plain_m.start()
    mine_p = project(top_rows, 1)
    opp_p.wait_recv()
    to_p[top_rows, :] = (mine_p + relay_p[...].astype(F32)).astype(BF16)
    sum_p.start()
    mine_m = project(low_rows, 3)
    opp_m.wait_recv()
    to_m[low_rows, :] = (mine_m + relay_m[...].astype(F32)).astype(BF16)
    sum_m.start()
    own_out = pltpu.make_async_copy(own_sum, o_ref, own_sem.at[0])
    mine_top = project(top_rows, 0)
    mine_low = project(low_rows, 0)
    plain_m.wait_recv()
    own_sum[top_rows, :] = mine_top + early_p[...].astype(F32)
    plain_p.wait_recv()
    own_sum[low_rows, :] = mine_low + early_m[...].astype(F32)
    own_out.start()
    own_out.wait()
    sum_p.wait_recv()
    sum_m.wait_recv()
    for copy in (opp_p, opp_m, plain_p, plain_m, sum_p, sum_m):
        copy.wait_send()
    @pl.when(place < n_ctx - 1)
    def _():
        for which in range(parts):
            own_hop(which).wait_send()

    def settle(step, _):
        @pl.when(onward(step))
        def _():
            for which in range(parts):
                hop(which, step).wait_send()
        return 0

    lax.fori_loop(1, hops, settle, 0)
    if detour:
        @pl.when(((col == 9) | (col == 10)) & (row < n_row - 1))
        def _():
            for which in range(parts):
                leave(which, 5).wait_send()

        @pl.when(((col == 5) | (col == 6) | (col == 1)) & (row > 0))
        def _():
            for which in range(parts):
                pass_last(which).wait_send()


def solution(mesh):
    n_ctx, n_head = mesh.shape["ctx"], mesh.shape["head"]
    n_x = n_head // 2

    def body(queries, keys, values, segment_ids, out_weight):
        tokens, width = queries.shape
        heads = width // HEAD_DIM
        hops = min(-(-(DOC_MAX - 1) // tokens), n_ctx - 1)
        half = tokens // 2
        parts = 1 + 2 * PIECES
        any_space = pl.BlockSpec(memory_space=pl.ANY)
        dma = pltpu.SemaphoreType.DMA
        own, late = pl.pallas_call(
            functools.partial(kernel, hops, n_ctx, n_x),
            out_shape=[jax.ShapeDtypeStruct((tokens, width), kind) for kind in (F32, BF16)],
            in_specs=[any_space] * 5,
            out_specs=[any_space] * 2,
            scratch_shapes=[
                pltpu.VMEM((tokens, width), BF16),
                pltpu.VMEM((tokens, HEAD_DIM), BF16),
                pltpu.VMEM((tokens, HEAD_DIM), BF16),
                pltpu.VMEM((1, tokens), jnp.int32),
                pltpu.VMEM((hops, tokens, HEAD_DIM), BF16),
                pltpu.VMEM((hops, tokens, HEAD_DIM), BF16),
                pltpu.VMEM((hops, 1, tokens), jnp.int32),
                pltpu.VMEM((n_x, 2 * width, width), BF16),
                pltpu.VMEM((tokens, 2 * width), BF16),
                pltpu.VMEM((heads, tokens, 2 * HEAD_DIM), F32),
                pltpu.VMEM((heads, tokens, HEAD_DIM), F32),
                pltpu.VMEM((tokens, width), BF16),
                pltpu.VMEM((tokens, width), BF16),
                pltpu.VMEM((tokens, width), BF16),
                pltpu.VMEM((half, width), BF16),
                pltpu.VMEM((half, width), BF16),
                pltpu.VMEM((half, width), BF16),
                pltpu.VMEM((half, width), BF16),
                pltpu.VMEM((tokens, width), F32),
                pltpu.VMEM((1, tokens), jnp.int32),
                pltpu.VMEM((tokens, HEAD_DIM), BF16),
                pltpu.VMEM((tokens, HEAD_DIM), BF16),
                pltpu.VMEM((heads, tokens, tokens), BF16),
                pltpu.VMEM((heads, tokens, HEAD_DIM), F32),
                dma((4,)),
                dma((n_x,)), dma((n_x,)), dma((n_x,)),
                dma((hops, parts)), dma((hops, parts)),
                dma((heads,)), dma((heads,)),
                dma((6,)), dma((6,)),
                dma((parts,)), dma((parts,)), dma((parts,)),
            ],
            compiler_params=pltpu.CompilerParams(collective_id=0, has_side_effects=True),
        )(queries, keys, values, segment_ids.reshape(1, tokens), out_weight)
        return (own + late.astype(F32)).astype(BF16)

    in_specs = (P("ctx", "head"), P("ctx", "head"), P("ctx", "head"), P("ctx"), P("head", None))
    return jax.shard_map(body, mesh=mesh, in_specs=in_specs, out_specs=P("ctx", "head"), check_vma=False)
```
